32 devices in a mesh: bfly: 32 (over z, y, x, core).
Axes of the slice: x: 2, y: 2, z: 4, core: 2. Of those that a mesh axis runs over, the one named last changes fastest.
Arguments:
- coeffs: float32 [32, 384, 1024], P('bfly'), may hold values from -6 to 6
- transfers: float32 [32, 8, 2, 384, 384], P('bfly'), may hold values from -0.21875 to 0.21875
Outputs:
- result: float32 [32, 384, 1024], P('bfly')
The draws below stay inside these ranges and needn't reach their ends.
All inputs are finite; a program needn't handle non-finite values.
Results may differ from the reference program's by a relative error of at most 0.00014.
Values sent between devices are 32-bit elements; how exact they have to be, the bound alone decides.
A program may use at most 64 MiB of HBM per device.

```python
import jax
import jax.numpy as jnp
from jax import lax

RANK = 384
COLS = 1024
LEVELS = 8
NODES = 32
N_BFLY = 32


def level_of(key, extent, shards, low, high):
    gain = 1.0
    for position, blocks in shards:
        draws = jax.random.uniform(jax.random.fold_in(jax.random.fold_in(key, 6), position), (blocks,), jnp.float32, low / len(shards), high / len(shards))
        gain = gain * jnp.repeat(jnp.exp(draws), extent[position] // blocks).reshape((-1,) + (1,) * (len(extent) - 1 - position))
    return gain


def scatter_about(key, shape, width, most, cuts=(), kind=jnp.bfloat16):
    values = jax.random.normal(key, shape, jnp.float32) * width
    if len(cuts) > 0:
        values = level_of(key, shape, cuts, -0.22, 0.18) * values
    return jnp.clip(values, min=-most, max=most).astype(kind)


def setup_inputs(seed: int = 0) -> dict:
    key_list = jax.random.split(jax.random.key(seed), 3)
    coeffs = scatter_about(key_list[0], (NODES, RANK, COLS), 1.0, 6.0, ((0, 32),), jnp.float32)
    transfers = scatter_about(key_list[1], (NODES, LEVELS, 2, RANK, RANK), (2 * RANK) ** -0.5, 0.21875, ((0, 32),), jnp.float32)
    return {"coeffs": coeffs, "transfers": transfers}


def reference(coeffs, transfers):
    bit_count = N_BFLY.bit_length() - 1
    node_ids = jnp.arange(N_BFLY, dtype=jnp.int32)
    state = coeffs
    for depth_level in range(LEVELS):
        bit_value = 1 << (depth_level % bit_count)
        partner = jnp.bitwise_xor(node_ids, bit_value).astype(jnp.int32)
        own_term = jnp.einsum("nij,njc->nic", transfers[:, depth_level, 0], state, precision=lax.Precision.HIGHEST)
        sent_term = jnp.einsum("nij,njc->nic", transfers[:, depth_level, 1], state, precision=lax.Precision.HIGHEST)
        state = own_term + sent_term[partner]
    return state
```

```python
import functools

import jax
import jax.numpy as jnp
from jax import lax
from jax.experimental import pallas as pl
from jax.experimental.pallas import tpu as pltpu
from jax.sharding import PartitionSpec as P

LANES = 128
ORDER = (8, 7, 6, 4, 5, 0, 1, 2, 3, -1)
LAG = (0, 1, 2, 3, 5, 6, 7, 8, 9)


def kernel(axis, bits, levels, chunks, coeffs, transfers, out, own, sent, got, raw, mats,
           in_sem, raw_sem, out_sem, send_sem, recv_sem):
    me = lax.axis_index(axis)
    rank = own.shape[1]

    def peer(level):
        step = 2 ** (level % bits)
        return me + step * (1 - 2 * ((me // step) % 2))

    def columns(c):
        return pl.ds(pl.multiple_of(c * LANES, LANES), LANES)

    def load_chunk(c):
        return pltpu.make_async_copy(coeffs.at[0, :, columns(c)], own.at[c], in_sem.at[c])

    def load_level(level):
        return pltpu.make_async_copy(transfers.at[0, level], raw.at[level], raw_sem.at[level])

    def store_chunk(c):
        return pltpu.make_async_copy(own.at[c], out.at[0, :, columns(c)], out_sem.at[c])

    def exchange(level, c):
        return pltpu.make_async_remote_copy(
            src_ref=sent.at[level, c],
            dst_ref=got.at[level, c],
            send_sem=send_sem.at[level, c],
            recv_sem=recv_sem.at[level, c],
            device_id=(peer(level),),
            device_id_type=pl.DeviceIdType.MESH,
        )

    barrier = pltpu.get_barrier_semaphore()
    for bit in range(min(bits, levels)):
        pl.semaphore_signal(barrier, inc=1, device_id=(peer(bit),),
                            device_id_type=pl.DeviceIdType.MESH)

    load_level(0).start()
    for c in range(chunks):
        load_chunk(c).start()
    for level in range(1, levels):
        load_level(level).start()

    def prepare(level):
        load_level(level).wait()
        for side in range(2):
            full = raw[level, side]
            high = full.astype(jnp.bfloat16)
            low = (full - high.astype(jnp.float32)).astype(jnp.bfloat16)
            mats[level, side, :, 0:rank] = high
            mats[level, side, :, rank:2 * rank] = low
            mats[level, side, :, 2 * rank:3 * rank] = high

    def apply(level, c):
        if level == 0:
            load_chunk(c).wait()
            state = own[c]
        else:
            exchange(level - 1, c).wait_recv()
            state = own[c] + got[level - 1, c]
        high = state.astype(jnp.bfloat16)
        low = (state - high.astype(jnp.float32)).astype(jnp.bfloat16)
        stack = jnp.concatenate([high, high, low], axis=0)
        sent[level, c] = jnp.dot(mats[level, 1], stack, preferred_element_type=jnp.float32)
        exchange(level, c).start()
        own[c] = jnp.dot(mats[level, 0], stack, preferred_element_type=jnp.float32)

    def finish(c):
        exchange(levels - 1, c).wait_recv()
        own[c] = own[c] + got[levels - 1, c]
        store_chunk(c).start()

    prepare(0)
    pl.semaphore_wait(barrier, min(bits, levels))

    def wave(w, carry):
        for part in ORDER:
            if part < 0:
                @pl.when(w < levels - 1)
                def _():
                    prepare(w + 1)
                continue
            c = w - LAG[part]

            @pl.when((c >= 0) & (c < chunks))
            def _():
                if part < levels:
                    apply(part, c)
                else:
                    finish(c)
        return carry

    lax.fori_loop(0, chunks + LAG[-1], wave, 0)

    def drain(c, carry):
        for level in range(levels):
            exchange(level, c).wait_send()
        store_chunk(c).wait()
        return carry

    lax.fori_loop(0, chunks, drain, 0)


def on_device(coeffs, transfers):
    bits = lax.axis_size("bfly").bit_length() - 1
    _, rank, cols = coeffs.shape
    levels = transfers.shape[1]
    chunks = cols // LANES
    f32, bf16 = jnp.float32, jnp.bfloat16
    return pl.pallas_call(
        functools.partial(kernel, "bfly", bits, levels, chunks),
        out_shape=jax.ShapeDtypeStruct(coeffs.shape, f32),
        in_specs=[pl.BlockSpec(memory_space=pl.ANY)] * 2,
        out_specs=pl.BlockSpec(memory_space=pl.ANY),
        scratch_shapes=[
            pltpu.VMEM((chunks, rank, LANES), f32),
            pltpu.VMEM((levels, chunks, rank, LANES), f32),
            pltpu.VMEM((levels, chunks, rank, LANES), f32),
            pltpu.VMEM((levels, 2, rank, rank), f32),
            pltpu.VMEM((levels, 2, rank, 3 * rank), bf16),
            pltpu.SemaphoreType.DMA((chunks,)),
            pltpu.SemaphoreType.DMA((levels,)),
            pltpu.SemaphoreType.DMA((chunks,)),
            pltpu.SemaphoreType.DMA((levels, chunks)),
            pltpu.SemaphoreType.DMA((levels, chunks)),
        ],
        compiler_params=pltpu.CompilerParams(
            collective_id=0, has_side_effects=True, vmem_limit_bytes=60 * 2**20
        ),
        name="butterfly",
    )(coeffs, transfers)


def solution(mesh):
    return jax.shard_map(
        on_device,
        mesh=mesh,
        in_specs=(P("bfly", None, None), P("bfly", None, None, None, None)),
        out_specs=P("bfly", None, None),
        check_vma=False,
    )
```
